32 devices in a mesh: dp: 8 (over z, x), mp: 4 (over y, core).
Axes of the slice: x: 2, y: 2, z: 4, core: 2. Of those that a mesh axis runs over, the one named last changes fastest.
Arguments:
- tokens: bfloat16 [3072, 8192], P('dp', 'mp'), may hold values from -6 to 6
- frozen_base_weight: bfloat16 [8192, 8192], P('mp', 'dp'), may hold values from -0.0625 to 0.0625
- tenant_down_factors: bfloat16 [16, 8192, 64], P('dp', 'mp'), may hold values from -0.0625 to 0.0625
- tenant_up_factors: bfloat16 [16, 8192, 64], P('dp', 'mp'), may hold values from -0.75 to 0.75
- cotangent: bfloat16 [3072, 8192], P('dp', 'mp'), may hold values from -6 to 6
- block_tenant_index: int32 [24], replicated, may hold values from 0 to 15
- ranks: int32 [16], replicated, may hold values from 8 to 64
Outputs:
- layer_out: bfloat16 [3072, 8192], P('dp', 'mp')
- input_grad: bfloat16 [3072, 8192], P('dp', 'mp')
- down_grad: float32 [16, 8192, 64], P('dp', 'mp')
- up_grad: float32 [16, 8192, 64], P('dp', 'mp')
The draws below stay inside these ranges and needn't reach their ends.
Inputs may be any that keep to these rules, and one draw needn't show every extreme that they name: `block_tenant_index`: tenant of each block of 128 consecutive rows; some tenants own many blocks, some none. `ranks`: rank columns at or past a tenant's rank are unused.
All inputs are finite; a program needn't handle non-finite values.
Results may differ from the reference program's by a relative error of at most 0.017.
Values may be sent and summed in bfloat16 or wider, within the bound.
No kernel may reach another device: no remote copies, remote signals or barrier semaphores. Data moves between devices by JAX's collectives and lax.ppermute only.
A program may use at most 128 MiB of HBM per device.

```python
import math
import jax
import jax.numpy as jnp
import numpy as np
from jax import lax

MODEL_WIDTH = 8192
PADDED_RANK = 64
BLOCK = 128
TENANT_TOTAL = 16
TOKENS = 3072
NBLK = 24
N_MP = 4


def with_ends(result, stream_key, least, largest):
    extent = result.shape
    index_at = [jax.random.randint(jax.random.fold_in(stream_key, axis), (), 0, extent[axis]) for axis in range(len(extent))]
    result = result.at[tuple(index_at)].set(least)
    longest = extent.index(max(extent))
    index_at[longest] = (index_at[longest] + 1) % extent[longest]
    return result.at[tuple(index_at)].set(largest)


def level_of(rng, extent, cuts, low, top_value):
    def one(axis_at, blocks):
        draws = jax.random.uniform(jax.random.fold_in(jax.random.fold_in(rng, 6), axis_at), (blocks,), jnp.float32, low / len(cuts), top_value / len(cuts))
        return jnp.repeat(jnp.exp(draws), extent[axis_at] // blocks).reshape((-1,) + (1,) * (len(extent) - axis_at - 1))

    factor_of = one(*cuts[0])
    for cut in cuts[1:]:
        factor_of = factor_of * one(*cut)
    return factor_of


def cumulative_ranks(count, slope):
    portions = [(1 << 20) // math.isqrt(rank ** slope) + 1 for rank in range(1, count + 1)]
    spread = 1 + sum(portions) // (1 << 30)
    return np.cumsum(np.array([max(1, weight // spread) for weight in portions]))


def ranked_ids(key, dims, amount, skew):
    listing = cumulative_ranks(amount, skew)
    pick = jax.random.randint(jax.random.fold_in(key, 1), dims, 0, int(listing[amount - 1]))
    standing = jnp.searchsorted(jnp.asarray(listing, jnp.int32), pick, side="right")
    return jax.random.permutation(jax.random.fold_in(key, 2), amount)[standing].astype(jnp.int32)


def normal_values(own_key, extent, spread, bound, cuts=(), held_as=jnp.bfloat16):
    entries = spread * jax.random.normal(own_key, extent, jnp.float32)
    if cuts:
        entries = entries * level_of(own_key, extent, cuts, -0.22, 0.18)
    return jnp.clip(entries, -bound, bound).astype(held_as)


def setup_inputs(seed: int = 0) -> dict:
    splits = jax.random.split(jax.random.key(seed), 8)
    tokens = normal_values(splits[0], (TOKENS, MODEL_WIDTH), 1.0, 6.0, ((0, 8), (1, 4)))
    frozen_base_weight = normal_values(splits[1], (MODEL_WIDTH, MODEL_WIDTH), MODEL_WIDTH ** -0.5, 0.0625, ((0, 4), (1, 8)))
    tenant_down_factors = normal_values(splits[2], (TENANT_TOTAL, MODEL_WIDTH, PADDED_RANK), MODEL_WIDTH ** -0.5, 0.0625, ((0, 8), (1, 4)))
    tenant_up_factors = normal_values(splits[3], (TENANT_TOTAL, MODEL_WIDTH, PADDED_RANK), PADDED_RANK ** -0.5, 0.75, ((0, 8), (1, 4)))
    cotangent = normal_values(splits[4], (TOKENS, MODEL_WIDTH), 1.0, 6.0, ((0, 8), (1, 4)))
    block_tenant_index = with_ends(ranked_ids(splits[5], (NBLK,), TENANT_TOTAL, 2), jax.random.fold_in(splits[5], 3), 0, TENANT_TOTAL - 1).astype(jnp.int32)
    ranks = with_ends(jax.random.randint(splits[6], (TENANT_TOTAL,), 8, PADDED_RANK + 1), jax.random.fold_in(splits[6], 1), 8, PADDED_RANK).astype(jnp.int32)
    return {"tokens": tokens, "frozen_base_weight": frozen_base_weight, "tenant_down_factors": tenant_down_factors, "tenant_up_factors": tenant_up_factors, "cotangent": cotangent, "block_tenant_index": block_tenant_index, "ranks": ranks}


def reference(tokens, frozen_base_weight, tenant_down_factors, tenant_up_factors, cotangent, block_tenant_index, ranks):
    count_of_tenants = tenant_down_factors.shape[0]
    block_total = block_tenant_index.shape[0]
    row_total = tokens.shape[0]
    positions = jnp.arange(PADDED_RANK, dtype=jnp.int32)
    kept = (positions[None, :] < ranks[:, None]).astype(jnp.float32)
    coef = kept * (16.0 / ranks.astype(jnp.float32))[:, None]
    block_coef = coef[block_tenant_index]
    tok_blocks = tokens.reshape(block_total, BLOCK, MODEL_WIDTH).astype(jnp.float32)
    cot_blocks = cotangent.reshape(block_total, BLOCK, MODEL_WIDTH).astype(jnp.float32)
    chosen_down_factor = tenant_down_factors[block_tenant_index].astype(jnp.float32)
    chosen_up_factor = tenant_up_factors[block_tenant_index].astype(jnp.float32)
    pre_low = jnp.einsum("bid,bdr->bir", tok_blocks, chosen_down_factor)
    low = (pre_low * block_coef[:, None, :]).astype(jnp.bfloat16)
    span = MODEL_WIDTH // N_MP
    base = jnp.zeros((row_total, MODEL_WIDTH), jnp.float32)
    for portion in range(N_MP):
        term = jnp.dot(tokens[:, portion * span:(portion + 1) * span],
                       frozen_base_weight[portion * span:(portion + 1) * span, :],
                       preferred_element_type=jnp.float32)
        rounded = lax.optimization_barrier(term.astype(jnp.bfloat16))
        base = base + rounded.astype(jnp.float32)
    adapter = jnp.einsum("bir,ber->bie", low.astype(jnp.float32), chosen_up_factor).reshape(row_total, MODEL_WIDTH)
    layer_out = (base + adapter).astype(jnp.bfloat16)
    pre_dlow = jnp.einsum("bie,ber->bir", cot_blocks, chosen_up_factor)
    dlow = (pre_dlow * block_coef[:, None, :]).astype(jnp.bfloat16)
    base_grad = jnp.dot(cotangent, frozen_base_weight.T, preferred_element_type=jnp.float32)
    adapter_grad = jnp.einsum("bir,bdr->bid", dlow.astype(jnp.float32), chosen_down_factor).reshape(row_total, MODEL_WIDTH)
    input_grad = (base_grad + adapter_grad).astype(jnp.bfloat16)
    block_down = jnp.einsum("bid,bir->bdr", tok_blocks, dlow.astype(jnp.float32))
    block_up = jnp.einsum("bie,bir->ber", cot_blocks, low.astype(jnp.float32))
    onehot = (block_tenant_index[None, :] == jnp.arange(count_of_tenants, dtype=jnp.int32)[:, None]).astype(jnp.float32)
    down_grad = jnp.einsum("tb,bdr->tdr", onehot, block_down, precision=lax.Precision.HIGHEST)
    up_grad = jnp.einsum("tb,ber->ter", onehot, block_up, precision=lax.Precision.HIGHEST)
    return layer_out, input_grad, down_grad, up_grad
```

```python
import jax
import jax.numpy as jnp
from jax import lax
from jax.sharding import PartitionSpec as P

BLOCK = 128
AXES = ("dp", "mp")
F32 = jnp.float32
BF16 = jnp.bfloat16


def dot(a, b, ca, cb):
    return lax.dot_general(a, b, (((ca,), (cb,)), ((), ())), preferred_element_type=F32)


def make_local(num_dp, num_mp):
    n = num_mp
    xs = num_dp // n
    cs = 2 if n % 2 == 0 else 1
    ys = n // cs

    def lin(z, x, y, c):
        return ((z * xs + x) * ys + y) * cs + c

    places = [
        (z, x, y, c) for z in range(n) for x in range(xs) for y in range(ys) for c in range(cs)
    ]

    def send(value, target):
        pairs = []
        for place in places:
            goal = target(*place)
            if goal is not None:
                pairs.append((lin(*place), lin(*goal)))
        return lax.ppermute(value, AXES, pairs)

    def kappa(y, c):
        return c * ys + y

    def to_group(z, x, y, c):
        m = y * cs + c
        k = (z - m) % n
        return (m, x, k % ys, k // ys)

    def to_home(z, x, y, c):
        return ((z + kappa(y, c)) % n, x, z // cs, z % cs)

    def local(tokens, weight, down, up, cotangent, block_tenant, ranks):
        dp = lax.axis_index("dp")
        mp = lax.axis_index("mp")
        z, x = dp // xs, dp % xs
        y, c = mp // cs, mp % cs
        rows, width = tokens.shape
        blocks = rows // BLOCK
        held, _, rank = down.shape
        piece = weight.shape[1]
        joined = xs * held
        kap = kappa(y, c)
        up_group = (z + kap) % n

        up_flat = up.transpose(1, 0, 2).reshape(width, held * rank)
        down_flat = down.transpose(1, 0, 2).reshape(width, held * rank)
        g_first = send(cotangent, to_group)
        up_first = send(up_flat, to_group)
        plus, minus = [tokens], [tokens]
        for s in range(1, n):
            plus.append(
                send(
                    plus[-1],
                    lambda z, x, y, c, s=s: (z + 1, x, y, c) if s - 1 <= z <= n - 2 else None,
                )
            )
            minus.append(
                send(
                    minus[-1],
                    lambda z, x, y, c, s=s: (z - 1, x, y, c) if 1 <= z <= n - s else None,
                )
            )

        def from_x(value):
            return [value] + [
                send(value, lambda z, x, y, c, s=s: (z, (x - s) % xs, y, c))
                for s in range(1, xs)
            ]

        w_parts = from_x(weight)
        w_tile = jnp.concatenate([weight] * xs, axis=1)
        for s in range(1, xs):
            w_tile = lax.dynamic_update_slice(w_tile, w_parts[s], (0, ((x + s) % xs) * piece))
        d_tile = jnp.concatenate(from_x(down_flat), axis=1)
        u_tile = jnp.concatenate(from_x(up_first), axis=1)
        near = [(x + s) % xs for s in range(xs)]
        tid_down = [(z * xs + near[s]) * held + h for s in range(xs) for h in range(held)]
        tid_up = [(up_group * xs + near[s]) * held + h for s in range(xs) for h in range(held)]

        tenant_count = ranks.shape[0]
        positions = jnp.arange(rank, dtype=jnp.int32)
        kept = (positions[None, :] < ranks[:, None]).astype(F32)
        coef_table = kept * (16.0 / ranks.astype(F32))[:, None]
        tenants, coefs = [], []
        for k in range(n):
            start = (((z + k) % n) * xs + x) * blocks
            own = lax.dynamic_slice_in_dim(block_tenant, start, blocks)
            onehot = (own[:, None] == jnp.arange(tenant_count, dtype=jnp.int32)[None, :]).astype(
                F32
            )
            coef = jnp.dot(onehot, coef_table, precision=lax.Precision.HIGHEST)
            coefs.append(
                jnp.broadcast_to(coef[:, None, :], (blocks, BLOCK, rank)).reshape(rows, rank)
            )
            tenants.append(
                jnp.broadcast_to(own[:, None], (blocks, BLOCK)).reshape(rows, 1)
            )

        def fold(wide, tenant, ids):
            total = None
            for j in range(joined):
                part = jnp.where(tenant == ids[j], wide[:, j * rank : (j + 1) * rank], 0.0)
                total = part if total is None else total + part
            return total

        def spread(thin, tenant, ids):
            return jnp.concatenate(
                [jnp.where(tenant == ids[j], thin, jnp.zeros_like(thin)) for j in range(joined)],
                axis=1,
            )

        half = n * rows // 2

        def pack(parts):
            whole = jnp.concatenate(parts, axis=0)
            return jnp.concatenate([whole[:half], whole[half:]], axis=1)

        def unpack(packed):
            return jnp.concatenate([packed[:, :rank], packed[:, rank:]], axis=0)

        def roll(whole, by):
            twice = jnp.concatenate([whole, whole], axis=0)
            return lax.dynamic_slice_in_dim(twice, by * rows, n * rows)

        def sum_mp(packed):
            total = packed
            if cs == 2:
                other = send(total.astype(BF16), lambda z, x, y, c: (z, x, y, 1 - c))
                total = total.astype(BF16).astype(F32) + other.astype(F32)
            mine = total.astype(BF16)
            for j in range(1, ys):
                other = send(mine, lambda z, x, y, c, j=j: (z, x, (y - j) % ys, c))
                total = total + other.astype(F32)
            return total

        by_shift = [g_first] + [
            send(g_first, lambda z, x, y, c, j=j: (z, x, (y - j) % ys, c)) for j in range(1, ys)
        ]
        g_slots = [None] * n
        for t in range(ys):
            at = (t - y) % ys
            mine = by_shift[0]
            for j in range(1, ys):
                mine = jnp.where(at == j, by_shift[j], mine)
            if cs == 2:
                other = send(mine, lambda z, x, y, c: (z, x, y, 1 - c))
                g_slots[t] = jnp.where(c == 0, mine, other)
                g_slots[ys + t] = jnp.where(c == 0, other, mine)
            else:
                g_slots[t] = mine

        x_slots = [tokens] + [jnp.where(z + k < n, minus[k], plus[n - k]) for k in range(1, n)]

        pre = [fold(dot(g_slots[k], u_tile, 1, 0), tenants[k], tid_up) for k in range(n)]
        pre = roll(jnp.concatenate(pre, axis=0).astype(BF16), kap)
        pre = jnp.concatenate([pre[:half], pre[half:]], axis=1)
        pre_dlow = unpack(sum_mp(send(pre, to_home).astype(F32)))
        dlow_wide = [
            spread(
                (pre_dlow[k * rows : (k + 1) * rows] * coefs[k]).astype(BF16),
                tenants[k],
                tid_down,
            )
            for k in range(n)
        ]

        pre = [fold(dot(x_slots[k], d_tile, 1, 0), tenants[k], tid_down) for k in range(n)]
        pre = send(sum_mp(pack(pre)).astype(BF16), to_group)
        pre_low = roll(unpack(pre), (n - kap) % n).astype(F32)
        low_wide = [
            spread(
                (pre_low[k * rows : (k + 1) * rows] * coefs[k]).astype(BF16),
                tenants[k],
                tid_up,
            )
            for k in range(n)
        ]

        parts = [
            dot(g_slots[k], w_tile, 1, 1) + dot(dlow_wide[k], d_tile, 1, 1) for k in range(n)
        ]
        parts = [lax.optimization_barrier(part.astype(BF16)) for part in parts]
        go_up = go_down = None
        for t in range(1, n):
            first, second = parts[n - t], parts[t]
            if t > 1:
                first = (first.astype(F32) + go_up.astype(F32)).astype(BF16)
                second = (second.astype(F32) + go_down.astype(F32)).astype(BF16)
            go_up = send(first, lambda z, x, y, c: (z + 1, x, y, c) if z < t else None)
            go_down = send(second, lambda z, x, y, c: (z - 1, x, y, c) if z >= n - t else None)
        input_grad = parts[0].astype(F32)
        if n > 1:
            input_grad = input_grad + go_up.astype(F32) + go_down.astype(F32)
        input_grad = input_grad.astype(BF16)

        main = [lax.optimization_barrier(dot(x_slots[k], w_tile, 1, 0)) for k in range(n)]
        shares = [
            (main[k] + dot(low_wide[k], u_tile, 1, 1)).astype(BF16) for k in range(n)
        ]
        if cs == 2:
            sums = []
            for t in range(ys):
                away = jnp.where(c == 0, shares[ys + t], shares[t])
                keep = jnp.where(c == 0, shares[t], shares[ys + t])
                other = send(away, lambda z, x, y, c: (z, x, y, 1 - c))
                sums.append((keep.astype(F32) + other.astype(F32)).astype(BF16))
        else:
            sums = shares

        def pick(index):
            value = sums[0]
            for t in range(1, ys):
                value = jnp.where(index == t, sums[t], value)
            return value

        total = pick(y).astype(F32)
        for j in range(1, ys):
            other = send(pick((y + j) % ys), lambda z, x, y, c, j=j: (z, x, (y + j) % ys, c))
            total = total + other.astype(F32)
        layer_out = send(total.astype(BF16), to_home)

        def reduce_x(wide):
            span = held * rank
            total = wide[:, :span]
            for s in range(1, xs):
                other = send(
                    wide[:, s * span : (s + 1) * span].astype(BF16),
                    lambda z, x, y, c, s=s: (z, (x + s) % xs, y, c),
                )
                total = total + other.astype(F32)
            return total

        down_sum = sum(dot(x_slots[k], dlow_wide[k], 0, 0) for k in range(n))
        up_sum = sum(dot(g_slots[k], low_wide[k], 0, 0) for k in range(n))
        down_grad = reduce_x(down_sum)
        up_grad = send(reduce_x(up_sum).astype(BF16), to_home).astype(F32)
        down_grad = down_grad.reshape(width, held, rank).transpose(1, 0, 2)
        up_grad = up_grad.reshape(width, held, rank).transpose(1, 0, 2)
        return layer_out, input_grad, down_grad, up_grad

    return local


def solution(mesh):
    return jax.shard_map(
        make_local(mesh.shape["dp"], mesh.shape["mp"]),
        mesh=mesh,
        in_specs=(
            P("dp", "mp"),
            P("mp", "dp"),
            P("dp", "mp", None),
            P("dp", "mp", None),
            P("dp", "mp"),
            P(),
            P(),
        ),
        out_specs=(P("dp", "mp"), P("dp", "mp"), P("dp", "mp", None), P("dp", "mp", None)),
        check_vma=False,
    )
```
